32 devices in a mesh: layer: 8 (over z, x), tile: 4 (over y, core).
Axes of the slice: x: 2, y: 2, z: 4, core: 2. Of those that a mesh axis runs over, the one named last changes fastest.
Arguments:
- source_modes: bfloat16 [8, 8, 2, 32, 512], P('layer', None, None, 'tile'), may hold values from -6 to 6
- port_cells: int32 [8], replicated, may hold values from 0 to 511
- frequencies: float32 [2], replicated, may hold values from 0.3 to 1.5, as said below
- layer_inverse: bfloat16 [8, 2, 32, 512, 512], P('layer', None, 'tile'), may hold values from -0.092807765 to 1.6928078
- coupling_self: float32 [8, 2, 32, 512], P('layer', None, 'tile'), may hold values from 0.4 to 1
- coupling_curl: float32 [8, 2, 32, 512], P('layer', None, 'tile'), may hold values from -4 to 4
Outputs:
- snapshot_basis: float32 [8, 32, 2, 32, 512], P('layer', None, None, 'tile')
- triangle: float32 [32, 32], replicated
The draws below stay inside these ranges and needn't reach their ends.
Inputs may be any that keep to these rules, and one draw needn't show every extreme that they name: `port_cells`: each port's profile is centred on this plane column. `frequencies`: the second frequency is 1.5 to 2.5 times the first.
All inputs are finite; a program needn't handle non-finite values.
Results may differ from the reference program's by a relative error of at most 0.04.
Values may be sent and summed in bfloat16 or wider, within the bound.
A program may use at most 64 MiB of HBM per device.

```python
import math
import jax
import jax.numpy as jnp
from jax import lax

PW = 512
NPORT = 8
NRHS = 32
NL = 8
PR = 32


def draw_layer_inverse(key, part):
    key_one, key_two = jax.random.split(jax.random.fold_in(key, 11))
    full_shape = (NL, 2, PR, PW, PW)
    jitter = jnp.clip(jax.random.normal(key_one, full_shape, jnp.float32), -4.0, 4.0)
    diagonal = jax.random.uniform(key_two, (NL, 2, PR, PW), jnp.float32, 1.0, 1.5)
    identity = (jnp.arange(PW)[:, None] == jnp.arange(PW)[None, :]).astype(jnp.float32)
    return (jitter * (0.5 / math.sqrt(PW)) + diagonal[..., None] * identity).astype(jnp.bfloat16)


def draw_frequencies(key, part):
    key_one, key_two = jax.random.split(jax.random.fold_in(key, 23))
    base = jnp.exp(jax.random.uniform(key_one, (), jnp.float32, math.log(0.3), math.log(0.6)))
    ratio = jnp.exp(jax.random.uniform(key_two, (), jnp.float32, math.log(1.5), math.log(2.5)))
    return jnp.stack([base, base * ratio]).astype(jnp.float32)


def set_ends(drawn, own_key, low, top_value):
    longest = drawn.shape.index(max(drawn.shape))
    spots = []
    for shift in (0, 1):
        where = [jax.random.randint(jax.random.fold_in(own_key, axis), (), 0, length) for axis, length in enumerate(drawn.shape)]
        where[longest] = (where[longest] + shift) % drawn.shape[longest]
        spots.append(tuple(where))
    return drawn.at[spots[0]].set(low).at[spots[1]].set(top_value)


def levels(stream_key, dims, pieces, smallest, high):
    gain = 1.0
    for axis_at, shards_of in pieces:
        draws = jax.random.uniform(jax.random.fold_in(jax.random.fold_in(stream_key, 6), axis_at), (shards_of,), jnp.float32, smallest / len(pieces), high / len(pieces))
        gain = gain * jnp.repeat(jnp.exp(draws), dims[axis_at] // shards_of).reshape((-1,) + (1,) * (len(dims) - 1 - axis_at))
    return gain


def noise(own_key, extent, scale, most, pieces=(), kind=jnp.bfloat16):
    array = jax.random.normal(own_key, extent, jnp.float32) * scale
    if len(pieces) > 0:
        array = levels(own_key, extent, pieces, -0.22, 0.18) * array
    return jnp.clip(array, min=-most, max=most).astype(kind)


def setup_inputs(seed: int = 0) -> dict:
    arg_keys = jax.random.split(jax.random.key(seed), 7)
    return {
        "source_modes": noise(arg_keys[0], (NL, NPORT, 2, PR, PW), 1.0, 6.0, ((0, 8), (3, 4))),
        "port_cells": set_ends(jax.random.randint(arg_keys[1], (NPORT,), 0, PW), jax.random.fold_in(arg_keys[1], 1), 0, PW - 1).astype(jnp.int32),
        "frequencies": draw_frequencies(jax.random.fold_in(arg_keys[6], 71), 0),
        "layer_inverse": draw_layer_inverse(jax.random.fold_in(arg_keys[6], 71), 0),
        "coupling_self": jnp.clip(0.4 + 0.6 * jax.random.uniform(arg_keys[4], (NL, 2, PR, PW), jnp.float32) ** levels(arg_keys[4], (NL, 2, PR, PW), ((0, 8), (2, 4)), -0.2, 0.2), 0.4, 1.0),
        "coupling_curl": noise(arg_keys[5], (NL, 2, PR, PW), 0.3, 4.0, ((0, 8), (2, 4)), jnp.float32),
    }


def lower_factor(gram):
    order = gram.shape[0]
    index_row = jnp.arange(order)

    def column_step(col_no, lower):
        unit = (index_row == col_no).astype(gram.dtype)
        column = jnp.dot(gram, unit, precision=lax.Precision.HIGHEST)
        lower_row = jnp.dot(unit, lower, precision=lax.Precision.HIGHEST)
        column = column - jnp.dot(lower, lower_row, precision=lax.Precision.HIGHEST)
        pivot = jnp.sqrt(jnp.sum(column * unit))
        scaled = jnp.where(index_row >= col_no, column / pivot, 0.0)
        return lower + scaled[:, None] * unit[None, :]
    return lax.fori_loop(0, order, column_step, jnp.zeros_like(gram))

def lower_inverse(lower):
    order = lower.shape[0]
    index_row = jnp.arange(order)

    def row_step(row_no, inverse):
        unit = (index_row == row_no).astype(lower.dtype)
        lower_row = jnp.dot(unit, lower, precision=lax.Precision.HIGHEST)
        pivot = jnp.sum(lower_row * unit)
        new_row = (unit - jnp.dot(lower_row, inverse, precision=lax.Precision.HIGHEST)) / pivot
        return inverse + unit[:, None] * new_row[None, :]
    return lax.fori_loop(0, order, row_step, jnp.zeros_like(lower))

def couple(field, self_w, curl_w):
    x_part = field[:, 0]
    y_part = field[:, 1]
    rows_pad = jnp.pad(y_part, ((0, 0), (1, 1), (0, 0)))
    row_diff = rows_pad[:, 2:] - rows_pad[:, :-2]
    cols_pad = jnp.pad(x_part, ((0, 0), (0, 0), (1, 1)))
    col_diff = cols_pad[:, :, 2:] - cols_pad[:, :, :-2]
    part_one = self_w[0] * x_part + curl_w[0] * row_diff
    part_two = self_w[1] * y_part + curl_w[1] * col_diff
    return jnp.stack([part_one, part_two], axis=1)

def apply_inverse(inverse_block, vectors):
    return jnp.einsum('crik,jcrk->jcri', inverse_block.astype(jnp.float32), vectors.astype(jnp.float32), precision=lax.Precision.HIGHEST)

def excitation(source_layer, port_taper, phase_pair):
    full_field = source_layer.astype(jnp.float32)[:, None, None] * port_taper[:, None, None, None, None, :] * phase_pair[None, :, :, None, None, None]
    return full_field.reshape((-1,) + source_layer.shape[1:])

def reference(source_modes, port_cells, frequencies, layer_inverse, coupling_self, coupling_curl):
    columns = jnp.arange(PW, dtype=jnp.float32)
    offsets = (columns[None, :] - port_cells.astype(jnp.float32)[:, None]) / (PW // 8)
    port_taper = 1.0 / (1.0 + offsets * offsets)
    down_list = []
    previous = jnp.zeros((NRHS, 2, PR, PW), jnp.bfloat16)
    for layer_no in range(NL):
        phase_angle = frequencies * (layer_no + 1.0)
        phase_pair = jnp.stack([jnp.cos(phase_angle), jnp.sin(phase_angle)], axis=1)
        forcing = excitation(source_modes[layer_no], port_taper, phase_pair)
        residue = (forcing - couple(previous.astype(jnp.float32), coupling_self[layer_no], coupling_curl[layer_no])).astype(jnp.bfloat16)
        current = apply_inverse(layer_inverse[layer_no], residue).astype(jnp.bfloat16)
        down_list.append(current)
        previous = current
    up_list = [None] * NL
    following = jnp.zeros((NRHS, 2, PR, PW), jnp.float32)
    for layer_no in range(NL - 1, -1, -1):
        up_image = couple(following, coupling_self[layer_no], coupling_curl[layer_no]).astype(jnp.bfloat16)
        update = apply_inverse(layer_inverse[layer_no], up_image)
        current = down_list[layer_no].astype(jnp.float32) - update
        up_list[layer_no] = current
        following = current
    snapshots = jnp.stack(up_list)
    columns_mat = jnp.moveaxis(snapshots, 1, 0).reshape(NRHS, -1)
    gram_whole = jnp.dot(columns_mat, columns_mat.T, precision=lax.Precision.HIGHEST)
    total_rows = NL * 2 * PR * PW
    lower = lower_factor(gram_whole / total_rows)
    triangle = lower.T
    solved = jnp.dot(lower_inverse(lower), columns_mat, precision=lax.Precision.HIGHEST)
    snapshot_basis = jnp.moveaxis(solved.reshape(NRHS, NL, 2, PR, PW), 0, 1)
    return (snapshot_basis, triangle)
```

```python
import functools

import jax
import jax.numpy as jnp
from jax import lax
from jax.experimental import pallas as pl
from jax.experimental.pallas import tpu as pltpu
from jax.sharding import PartitionSpec as P

MESH = pl.DeviceIdType.MESH
GROUPS = 4


def dot_last(a, b, precision=None):
    return lax.dot_general(
        a, b, (((1,), (1,)), ((), ())), precision=precision, preferred_element_type=jnp.float32
    )


def sweep_kernel(
    layers, tiles,
    src, weight_cols, self_w, curl_w, inv_hbm,
    snap, gram,
    inv, forcing, down_in, down, up_in, up_out, gram_acc, gram_tile, gram_layer, gram_part,
    inv_sem, down_send, down_recv, down_edge_send, down_edge_recv,
    up_send, up_recv, up_edge_send, up_edge_recv,
    tile_send, tile_recv, layer_send, layer_recv,
):
    layer = lax.axis_index("layer")
    tile = lax.axis_index("tile")
    groups, rows = down.shape[0], down.shape[1]
    width = down.shape[3]
    last = rows - 1
    odd = lax.rem(tile, 2)
    sign = 1 - 2 * odd
    front = tile - sign
    back = tile + sign
    has_front = jnp.logical_and(front >= 0, front < tiles)
    has_back = jnp.logical_and(back >= 0, back < tiles)
    partners = ((has_front, front), (has_back, back))
    top = layers - 1
    not_first = layer > 0
    not_last = layer < top

    def row_of(step):
        return step + odd * (last - 2 * step)

    def inv_copy(comp, step):
        row = row_of(step)
        return pltpu.make_async_copy(
            inv_hbm.at[0, comp, row], inv.at[comp, row], inv_sem.at[comp, step]
        )

    def start_weights(step, carry):
        inv_copy(0, step).start()
        inv_copy(1, step).start()
        return carry

    lax.fori_loop(0, rows, start_weights, 0)

    barrier = pltpu.get_barrier_semaphore()

    def greet(dev_layer, dev_tile):
        pl.semaphore_signal(barrier, inc=1, device_id=(dev_layer, dev_tile), device_id_type=MESH)

    for shift in (-1, 1):
        near = layer + shift
        ok = jnp.logical_and(near >= 0, near < layers)
        for has, partner in partners:
            @pl.when(jnp.logical_and(ok, has))
            def _(near=near, partner=partner):
                greet(near, partner)

    for k in range(1, layers):
        greet(lax.rem(layer + k, layers), tile)
    for k in range(1, tiles):
        greet(layer, lax.rem(tile + k, tiles))

    port_cols = width // 2
    row_no = lax.broadcasted_iota(jnp.int32, (width, src.shape[4]), 0)

    def make_forcing(group, carry):
        scale = weight_cols[group]
        for comp in range(2):
            first = src[0, 2 * group, comp].astype(jnp.float32)
            second = src[0, 2 * group + 1, comp].astype(jnp.float32)
            for row in range(rows):
                pair = jnp.where(row_no < port_cols, first[row : row + 1], second[row : row + 1])
                forcing[group, comp, row] = pair * scale
        return carry

    lax.fori_loop(0, groups, make_forcing, 0)

    @pl.when(layer == 0)
    def _():
        def clear(group, carry):
            down_in[group] = jnp.zeros(down_in.shape[1:], down_in.dtype)
            return carry

        lax.fori_loop(0, groups, clear, 0)

    for edge, (has, _) in enumerate(partners):
        slot = 0 if edge == 0 else rows + 1

        @pl.when(jnp.logical_not(has))
        def _(slot=slot):
            def clear(group, carry):
                down_in[group, slot, 1] = jnp.zeros(down_in.shape[3:], down_in.dtype)
                up_in[group, slot, 1] = jnp.zeros(up_in.shape[3:], up_in.dtype)
                return carry

            lax.fori_loop(0, groups, clear, 0)

    gram_acc[...] = jnp.zeros_like(gram_acc)

    sides = (layer > 0).astype(jnp.int32) + (layer < top).astype(jnp.int32)
    fronts = has_front.astype(jnp.int32) + has_back.astype(jnp.int32)
    pl.semaphore_wait(barrier, layers - 1 + tiles - 1 + sides * fronts)

    def main_copy(source, target, sems, group, step, near):
        return pltpu.make_async_remote_copy(
            src_ref=source.at[group, step], dst_ref=target.at[group, step + 1],
            send_sem=sems[0].at[group, step], recv_sem=sems[1].at[group, step],
            device_id=(near, tile), device_id_type=MESH,
        )

    def edge_copy(source, target, sems, group, edge, near):
        step, slot = (0, 0) if edge == 0 else (last, rows + 1)
        return pltpu.make_async_remote_copy(
            src_ref=source.at[group, step, 1], dst_ref=target.at[group, slot, 1],
            send_sem=sems[2].at[group, edge], recv_sem=sems[3].at[group, edge],
            device_id=(near, partners[edge][1]), device_id_type=MESH,
        )

    def send_unit(source, target, sems, group, step, near):
        main_copy(source, target, sems, group, step, near).start()
        for edge, at in ((0, 0), (1, last)):
            @pl.when(jnp.logical_and(step == at, partners[edge][0]))
            def _(edge=edge):
                edge_copy(source, target, sems, group, edge, near).start()

    def wait_unit(source, target, sems, group, step, near):
        @pl.when(step == 0)
        def _():
            main_copy(source, target, sems, group, 0, near).wait_recv()

            @pl.when(has_front)
            def _():
                edge_copy(source, target, sems, group, 0, near).wait_recv()

        @pl.when(step < last)
        def _():
            main_copy(source, target, sems, group, step + 1, near).wait_recv()

        @pl.when(jnp.logical_and(step == last, has_back))
        def _():
            edge_copy(source, target, sems, group, 1, near).wait_recv()

    def wait_sent(source, target, sems, near):
        def group_body(group, carry):
            def step_body(step, inner):
                main_copy(source, target, sems, group, step, near).wait_send()
                return inner

            lax.fori_loop(0, rows, step_body, 0)
            for edge in range(2):
                @pl.when(partners[edge][0])
                def _(edge=edge):
                    edge_copy(source, target, sems, group, edge, near).wait_send()

            return carry

        lax.fori_loop(0, groups, group_body, 0)

    down_sems = (down_send, down_recv, down_edge_send, down_edge_recv)
    up_sems = (up_send, up_recv, up_edge_send, up_edge_recv)
    plane_width = src.shape[4]
    lane = lax.broadcasted_iota(jnp.int32, (width, plane_width), 1)
    sign_f = sign.astype(jnp.float32)

    def couple(field, group, step, row):
        x_part = field[group, step + 1, 0].astype(jnp.float32)
        y_part = field[group, step + 1, 1].astype(jnp.float32)
        before = field[group, step, 1].astype(jnp.float32)
        after = field[group, step + 2, 1].astype(jnp.float32)
        row_diff = sign_f * (after - before)
        right = jnp.where(lane == plane_width - 1, 0.0, pltpu.roll(x_part, plane_width - 1, 1))
        left = jnp.where(lane == 0, 0.0, pltpu.roll(x_part, 1, 1))
        at = pl.ds(row, 1)
        part_one = self_w[0, 0, at, :] * x_part + curl_w[0, 0, at, :] * row_diff
        part_two = self_w[0, 1, at, :] * y_part + curl_w[0, 1, at, :] * (right - left)
        return part_one, part_two

    def columns_of(group):
        return pl.ds(pl.multiple_of(group * width, width), width)

    def add_gram(group, row):
        @pl.when(group == groups - 1)
        def _():
            for comp in range(2):
                block = snap[comp, row]
                gram_acc[:, : block.shape[0]] += dot_last(block, block, lax.Precision.HIGHEST)

    def down_unit(group, step):
        row = row_of(step)

        @pl.when(not_first)
        def _():
            wait_unit(down, down_in, down_sems, group, step, layer - 1)

        @pl.when(group == 0)
        def _():
            inv_copy(0, step).wait()
            inv_copy(1, step).wait()

        parts = couple(down_in, group, step, row)
        fields = []
        for comp in range(2):
            residue = (forcing[group, comp, row] - parts[comp]).astype(jnp.bfloat16)
            field = dot_last(residue, inv[comp, row]).astype(jnp.bfloat16)
            down[group, step, comp] = field
            fields.append(field)

        @pl.when(not_last)
        def _():
            send_unit(down, down_in, down_sems, group, step, layer + 1)

        @pl.when(layer == top)
        def _():
            if layers > 1:
                send_unit(down, up_in, up_sems, group, step, layer - 1)
            for comp in range(2):
                snap[comp, row, columns_of(group), :] = fields[comp].astype(jnp.float32)
            add_gram(group, row)

    def up_unit(group, step):
        row = row_of(step)
        wait_unit(up_out, up_in, up_sems, group, step, layer + 1)
        parts = couple(up_in, group, step, row)
        for comp in range(2):
            image = parts[comp].astype(jnp.bfloat16)
            update = dot_last(image, inv[comp, row])
            value = down[group, step, comp].astype(jnp.float32) - update
            snap[comp, row, columns_of(group), :] = value
            up_out[group, step, comp] = value.astype(jnp.bfloat16)

        @pl.when(not_first)
        def _():
            send_unit(up_out, up_in, up_sems, group, step, layer - 1)

        add_gram(group, row)

    def run(unit):
        def group_body(group, carry):
            def step_body(step, inner):
                unit(group, step)
                return inner

            return lax.fori_loop(0, rows, step_body, carry)

        lax.fori_loop(0, groups, group_body, 0)

    run(down_unit)

    @pl.when(not_last)
    def _():
        run(up_unit)

    gram_tile[tile] = gram_acc[...]
    for k in range(1, tiles):
        tile_copy(gram_acc, gram_tile, tile_send, tile_recv, k, tiles, layer, tile).start()
    for k in range(1, tiles):
        tile_copy(gram_acc, gram_tile, tile_send, tile_recv, k, tiles, layer, tile).wait_recv()
    gram_part[...] = functools.reduce(lambda a, b: a + b, [gram_tile[k] for k in range(tiles)])
    gram_layer[layer] = gram_part[...]
    for k in range(1, layers):
        layer_copy(gram_part, gram_layer, layer_send, layer_recv, k, layers, layer, tile).start()
    for k in range(1, layers):
        layer_copy(gram_part, gram_layer, layer_send, layer_recv, k, layers, layer, tile).wait_recv()
    gram[...] = functools.reduce(lambda a, b: a + b, [gram_layer[k] for k in range(layers)])

    for k in range(1, tiles):
        tile_copy(gram_acc, gram_tile, tile_send, tile_recv, k, tiles, layer, tile).wait_send()
    for k in range(1, layers):
        layer_copy(gram_part, gram_layer, layer_send, layer_recv, k, layers, layer, tile).wait_send()

    @pl.when(not_last)
    def _():
        wait_sent(down, down_in, down_sems, layer + 1)

    if layers > 1:
        @pl.when(layer == top)
        def _():
            wait_sent(down, up_in, up_sems, layer - 1)

    @pl.when(jnp.logical_and(not_first, not_last))
    def _():
        wait_sent(up_out, up_in, up_sems, layer - 1)


def tile_copy(source, target, send, recv, k, tiles, layer, tile):
    return pltpu.make_async_remote_copy(
        src_ref=source, dst_ref=target.at[tile], send_sem=send.at[k], recv_sem=recv.at[k],
        device_id=(layer, lax.rem(tile + k, tiles)), device_id_type=MESH,
    )


def layer_copy(source, target, send, recv, k, layers, layer, tile):
    return pltpu.make_async_remote_copy(
        src_ref=source, dst_ref=target.at[layer], send_sem=send.at[k], recv_sem=recv.at[k],
        device_id=(lax.rem(layer + k, layers), tile), device_id_type=MESH,
    )


def basis_kernel(total_rows, snap, gram, basis, triangle):
    order = triangle.shape[0]
    row_no = lax.broadcasted_iota(jnp.int32, gram.shape, 0)
    col_no = lax.broadcasted_iota(jnp.int32, gram.shape, 1)
    work = jnp.where(col_no < order, gram[...] / total_rows, 0.0)
    work = jnp.where(col_no == row_no + order, 1.0, work)
    for k in range(order):
        pivot = 1.0 / jnp.sqrt(work[k : k + 1, k : k + 1])
        line = work[k : k + 1, :] * pivot
        column = work[:, k : k + 1] * pivot
        below = work - column * line
        work = jnp.where(row_no > k, below, jnp.where(row_no == k, line, work))
    upper = jnp.where(col_no >= row_no, work, 0.0)
    triangle[...] = upper[:, :order]
    lower_inv = work[:, order : 2 * order]
    for comp in range(basis.shape[2]):
        for row in range(basis.shape[3]):
            solved = jnp.dot(
                lower_inv, snap[comp, row], precision=lax.Precision.HIGHEST,
                preferred_element_type=jnp.float32,
            )
            basis[0, :, comp, row, :] = solved


def per_device(source_modes, port_cells, frequencies, layer_inverse, coupling_self, coupling_curl):
    layers = lax.axis_size("layer")
    tiles = lax.axis_size("tile")
    layer_pos = lax.axis_index("layer")
    ports = source_modes.shape[1]
    rows = source_modes.shape[3]
    plane_width = source_modes.shape[4]
    order = ports * frequencies.shape[0] * 2
    groups = GROUPS
    width = order // groups
    columns = jnp.arange(plane_width, dtype=jnp.float32)
    offsets = (columns[None, :] - port_cells.astype(jnp.float32)[:, None]) / (plane_width // 8)
    port_taper = 1.0 / (1.0 + offsets * offsets)
    phase_angle = frequencies * (layer_pos + 1).astype(jnp.float32)
    phase_pair = jnp.stack([jnp.cos(phase_angle), jnp.sin(phase_angle)], axis=1)
    weight_cols = port_taper[:, None, :] * phase_pair.reshape(1, -1, 1)
    weight_cols = weight_cols.reshape(groups, width, plane_width)

    vmem = pl.BlockSpec(memory_space=pltpu.VMEM)
    dma = pltpu.SemaphoreType.DMA
    bf16, f32 = jnp.bfloat16, jnp.float32
    halo_shape = (groups, rows + 2, 2, width, plane_width)
    field_shape = (groups, rows, 2, width, plane_width)
    snap, gram = pl.pallas_call(
        functools.partial(sweep_kernel, layers, tiles),
        out_shape=(
            jax.ShapeDtypeStruct((2, rows, order, plane_width), f32),
            jax.ShapeDtypeStruct((order, 128), f32),
        ),
        in_specs=[vmem, vmem, vmem, vmem, pl.BlockSpec(memory_space=pl.ANY)],
        out_specs=(vmem, vmem),
        scratch_shapes=[
            pltpu.VMEM(layer_inverse.shape[1:], bf16),
            pltpu.VMEM((groups, 2, rows, width, plane_width), f32),
            pltpu.VMEM(halo_shape, bf16),
            pltpu.VMEM(field_shape, bf16),
            pltpu.VMEM(halo_shape, bf16),
            pltpu.VMEM(field_shape, bf16),
            pltpu.VMEM((order, 128), f32),
            pltpu.VMEM((tiles, order, 128), f32),
            pltpu.VMEM((layers, order, 128), f32),
            pltpu.VMEM((order, 128), f32),
            dma((2, rows)),
            dma((groups, rows)), dma((groups, rows)), dma((groups, 2)), dma((groups, 2)),
            dma((groups, rows)), dma((groups, rows)), dma((groups, 2)), dma((groups, 2)),
            dma((tiles,)), dma((tiles,)), dma((layers,)), dma((layers,)),
        ],
        compiler_params=pltpu.CompilerParams(collective_id=0, has_side_effects=True),
        name="sweep",
    )(source_modes, weight_cols, coupling_self, coupling_curl, layer_inverse)
    total_rows = layers * tiles * 2 * rows * plane_width
    return pl.pallas_call(
        functools.partial(basis_kernel, total_rows),
        out_shape=(
            jax.ShapeDtypeStruct((1, order, 2, rows, plane_width), f32),
            jax.ShapeDtypeStruct((order, order), f32),
        ),
        in_specs=[vmem, vmem],
        out_specs=(vmem, vmem),
        name="basis",
    )(snap, gram)


def solution(mesh):
    in_specs = (
        P("layer", None, None, "tile", None),
        P(),
        P(),
        P("layer", None, "tile", None, None),
        P("layer", None, "tile", None),
        P("layer", None, "tile", None),
    )
    out_specs = (P("layer", None, None, "tile", None), P())
    return jax.shard_map(
        per_device, mesh=mesh, in_specs=in_specs, out_specs=out_specs, check_vma=False
    )
```

```python
import functools

import jax
import jax.numpy as jnp
from jax import lax
from jax.experimental import pallas as pl
from jax.experimental.pallas import tpu as pltpu
from jax.sharding import PartitionSpec as P

MESH = pl.DeviceIdType.MESH
GROUPS = 4
TURN = 128
SPLIT = 2


def dot_last(a, b, precision=None):
    return lax.dot_general(
        a, b, (((1,), (1,)), ((), ())), precision=precision, preferred_element_type=jnp.float32
    )


def sweep_kernel(
    layers, tiles,
    port_cells, frequencies, src, self_w, curl_w, inv_hbm,
    snap, gram,
    inv, inv_t, forcing, down_in, down, up_in, up_out, gram_acc, gram_tile, gram_layer, gram_part,
    inv_sem, down_send, down_recv, down_edge_send, down_edge_recv,
    up_send, up_recv, up_edge_send, up_edge_recv,
    tile_send, tile_recv, layer_send, layer_recv,
):
    layer = lax.axis_index("layer")
    tile = lax.axis_index("tile")
    groups, rows = down.shape[0], down.shape[1]
    width = down.shape[3]
    last = rows - 1
    odd = lax.rem(tile, 2)
    sign = 1 - 2 * odd
    front = tile - sign
    back = tile + sign
    has_front = jnp.logical_and(front >= 0, front < tiles)
    has_back = jnp.logical_and(back >= 0, back < tiles)
    partners = ((has_front, front), (has_back, back))
    top = layers - 1
    not_first = layer > 0
    not_last = layer < top

    def row_of(step):
        return step + odd * (last - 2 * step)

    def inv_copy(comp, step):
        row = row_of(step)
        return pltpu.make_async_copy(
            inv_hbm.at[0, comp, row], inv.at[comp, row], inv_sem.at[comp, step]
        )

    def start_weights(step, carry):
        inv_copy(0, step).start()
        inv_copy(1, step).start()
        return carry

    lax.fori_loop(0, rows, start_weights, 0)

    barrier = pltpu.get_barrier_semaphore()

    def greet(dev_layer, dev_tile):
        pl.semaphore_signal(barrier, inc=1, device_id=(dev_layer, dev_tile), device_id_type=MESH)

    for shift in (-1, 1):
        near = layer + shift
        ok = jnp.logical_and(near >= 0, near < layers)
        for has, partner in partners:
            @pl.when(jnp.logical_and(ok, has))
            def _(near=near, partner=partner):
                greet(near, partner)

    for k in range(1, layers):
        greet(lax.rem(layer + k, layers), tile)
    for k in range(1, tiles):
        greet(layer, lax.rem(tile + k, tiles))

    plane_width = src.shape[4]
    row_no = lax.broadcasted_iota(jnp.int32, (width, plane_width), 0)
    lane = lax.broadcasted_iota(jnp.int32, (width, plane_width), 1)
    port_count = src.shape[1] // groups
    port_cols = width // port_count
    column = lane.astype(jnp.float32)
    in_port = lax.rem(row_no, port_cols)
    pitch = (layer + 1).astype(jnp.float32)
    angle = jnp.full((width, plane_width), frequencies[0] * pitch)
    for k in range(1, port_cols // 2):
        angle = jnp.where(in_port >= 2 * k, frequencies[k] * pitch, angle)
    phase = jnp.where(lax.rem(in_port, 2) == 0, jnp.cos(angle), jnp.sin(angle))

    def make_forcing(group, carry):
        centre = jnp.full((width, plane_width), port_cells[port_count * group].astype(jnp.float32))
        for k in range(1, port_count):
            cell = port_cells[port_count * group + k].astype(jnp.float32)
            centre = jnp.where(row_no >= k * port_cols, cell, centre)
        offset = (column - centre) / (plane_width // 8)
        scale = phase * (1.0 / (1.0 + offset * offset))
        for comp in range(2):
            modes = [src[0, port_count * group + k, comp].astype(jnp.float32) for k in range(port_count)]
            for row in range(rows):
                mixed = jnp.broadcast_to(modes[0][row : row + 1], scale.shape)
                for k in range(1, port_count):
                    mixed = jnp.where(row_no >= k * port_cols, modes[k][row : row + 1], mixed)
                forcing[group, comp, row] = mixed * scale
        return carry

    lax.fori_loop(0, groups, make_forcing, 0)

    @pl.when(layer == 0)
    def _():
        def clear(group, carry):
            down_in[group] = jnp.zeros(down_in.shape[1:], down_in.dtype)
            return carry

        lax.fori_loop(0, groups, clear, 0)

    for edge, (has, _) in enumerate(partners):
        slot = 0 if edge == 0 else rows + 1

        @pl.when(jnp.logical_not(has))
        def _(slot=slot):
            def clear(group, carry):
                down_in[group, slot, 1] = jnp.zeros(down_in.shape[3:], down_in.dtype)
                up_in[group, slot, 1] = jnp.zeros(up_in.shape[3:], up_in.dtype)
                return carry

            lax.fori_loop(0, groups, clear, 0)

    gram_acc[...] = jnp.zeros_like(gram_acc)

    sides = (layer > 0).astype(jnp.int32) + (layer < top).astype(jnp.int32)
    fronts = has_front.astype(jnp.int32) + has_back.astype(jnp.int32)
    pl.semaphore_wait(barrier, layers - 1 + tiles - 1 + sides * fronts)

    def main_copy(source, target, sems, group, step, near):
        return pltpu.make_async_remote_copy(
            src_ref=source.at[group, step], dst_ref=target.at[group, step + 1],
            send_sem=sems[0].at[group, step], recv_sem=sems[1].at[group, step],
            device_id=(near, tile), device_id_type=MESH,
        )

    def edge_copy(source, target, sems, group, edge, near):
        step, slot = (0, 0) if edge == 0 else (last, rows + 1)
        return pltpu.make_async_remote_copy(
            src_ref=source.at[group, step, 1], dst_ref=target.at[group, slot, 1],
            send_sem=sems[2].at[group, edge], recv_sem=sems[3].at[group, edge],
            device_id=(near, partners[edge][1]), device_id_type=MESH,
        )

    def send_unit(source, target, sems, group, step, near):
        main_copy(source, target, sems, group, step, near).start()
        for edge, at in ((0, 0), (1, last)):
            @pl.when(jnp.logical_and(step == at, partners[edge][0]))
            def _(edge=edge):
                edge_copy(source, target, sems, group, edge, near).start()

    def wait_unit(source, target, sems, group, step, near):
        @pl.when(step == 0)
        def _():
            main_copy(source, target, sems, group, 0, near).wait_recv()

            @pl.when(has_front)
            def _():
                edge_copy(source, target, sems, group, 0, near).wait_recv()

        @pl.when(step < last)
        def _():
            main_copy(source, target, sems, group, step + 1, near).wait_recv()

        @pl.when(jnp.logical_and(step == last, has_back))
        def _():
            edge_copy(source, target, sems, group, 1, near).wait_recv()

    def wait_sent(source, target, sems, near):
        def group_body(group, carry):
            def step_body(step, inner):
                main_copy(source, target, sems, group, step, near).wait_send()
                return inner

            lax.fori_loop(0, rows, step_body, 0)
            for edge in range(2):
                @pl.when(partners[edge][0])
                def _(edge=edge):
                    edge_copy(source, target, sems, group, edge, near).wait_send()

            return carry

        lax.fori_loop(0, groups, group_body, 0)

    down_sems = (down_send, down_recv, down_edge_send, down_edge_recv)
    up_sems = (up_send, up_recv, up_edge_send, up_edge_recv)
    sign_f = sign.astype(jnp.float32)

    def couple(field, group, step, row):
        x_part = field[group, step + 1, 0].astype(jnp.float32)
        y_part = field[group, step + 1, 1].astype(jnp.float32)
        before = field[group, step, 1].astype(jnp.float32)
        after = field[group, step + 2, 1].astype(jnp.float32)
        row_diff = sign_f * (after - before)
        right = jnp.where(lane == plane_width - 1, 0.0, pltpu.roll(x_part, plane_width - 1, 1))
        left = jnp.where(lane == 0, 0.0, pltpu.roll(x_part, 1, 1))
        at = pl.ds(row, 1)
        part_one = self_w[0, 0, at, :] * x_part + curl_w[0, 0, at, :] * row_diff
        part_two = self_w[0, 1, at, :] * y_part + curl_w[0, 1, at, :] * (right - left)
        return part_one, part_two

    def columns_of(group):
        return pl.ds(pl.multiple_of(group * width, width), width)

    def add_gram(group, row):
        @pl.when(group == groups - 1)
        def _():
            for comp in range(2):
                block = snap[comp, row]
                gram_acc[:, : block.shape[0]] += dot_last(block, block, lax.Precision.HIGHEST)

    def turn_block(comp, row):
        for at in range(0, plane_width, TURN):
            for to in range(0, plane_width, TURN):
                block = inv[comp, row, at : at + TURN, to : to + TURN]
                inv_t[comp, row, to : to + TURN, at : at + TURN] = block.T

    def apply_turned(vectors, comp, row):
        return jnp.dot(vectors, inv_t[comp, row], preferred_element_type=jnp.float32)

    def down_unit(opening, group, step):
        row = row_of(step)

        @pl.when(not_first)
        def _():
            wait_unit(down, down_in, down_sems, group, step, layer - 1)

        if opening:
            inv_copy(0, step).wait()
            inv_copy(1, step).wait()

        parts = couple(down_in, group, step, row)
        fields = []
        for comp in range(2):
            residue = (forcing[group, comp, row] - parts[comp]).astype(jnp.bfloat16)
            if opening:
                field = dot_last(residue, inv[comp, row]).astype(jnp.bfloat16)
            else:
                field = apply_turned(residue, comp, row).astype(jnp.bfloat16)
            down[group, step, comp] = field
            fields.append(field)
        if opening:
            for comp in range(2):
                turn_block(comp, row)

        @pl.when(not_last)
        def _():
            send_unit(down, down_in, down_sems, group, step, layer + 1)

        @pl.when(layer == top)
        def _():
            if layers > 1:
                send_unit(down, up_in, up_sems, group, step, layer - 1)
            for comp in range(2):
                snap[comp, row, columns_of(group), :] = fields[comp].astype(jnp.float32)
            add_gram(group, row)

    def up_unit(group, step):
        row = row_of(step)
        wait_unit(up_out, up_in, up_sems, group, step, layer + 1)
        parts = couple(up_in, group, step, row)
        for comp in range(2):
            image = parts[comp].astype(jnp.bfloat16)
            update = apply_turned(image, comp, row)
            value = down[group, step, comp].astype(jnp.float32) - update
            snap[comp, row, columns_of(group), :] = value
            up_out[group, step, comp] = value.astype(jnp.bfloat16)

        @pl.when(not_first)
        def _():
            send_unit(up_out, up_in, up_sems, group, step, layer - 1)

        add_gram(group, row)

    def run(unit, first):
        def group_body(group, carry):
            def step_body(step, inner):
                unit(group, step)
                return inner

            return lax.fori_loop(0, rows, step_body, carry)

        lax.fori_loop(first, groups, group_body, 0)

    def open_body(step, carry):
        down_unit(True, 0, step)
        return carry

    lax.fori_loop(0, rows, open_body, 0)
    run(functools.partial(down_unit, False), 1)

    @pl.when(not_last)
    def _():
        run(up_unit, 0)

    gram_tile[tile] = gram_acc[...]
    for k in range(1, tiles):
        tile_copy(gram_acc, gram_tile, tile_send, tile_recv, k, tiles, layer, tile).start()
    for k in range(1, tiles):
        tile_copy(gram_acc, gram_tile, tile_send, tile_recv, k, tiles, layer, tile).wait_recv()
    gram_part[...] = functools.reduce(lambda a, b: a + b, [gram_tile[k] for k in range(tiles)])
    gram_layer[layer] = gram_part[...]
    for k in range(1, layers):
        layer_copy(gram_part, gram_layer, layer_send, layer_recv, k, layers, layer, tile).start()
    for k in range(1, layers):
        layer_copy(gram_part, gram_layer, layer_send, layer_recv, k, layers, layer, tile).wait_recv()
    gram[...] = functools.reduce(lambda a, b: a + b, [gram_layer[k] for k in range(layers)])

    for k in range(1, tiles):
        tile_copy(gram_acc, gram_tile, tile_send, tile_recv, k, tiles, layer, tile).wait_send()
    for k in range(1, layers):
        layer_copy(gram_part, gram_layer, layer_send, layer_recv, k, layers, layer, tile).wait_send()

    @pl.when(not_last)
    def _():
        wait_sent(down, down_in, down_sems, layer + 1)

    if layers > 1:
        @pl.when(layer == top)
        def _():
            wait_sent(down, up_in, up_sems, layer - 1)

    @pl.when(jnp.logical_and(not_first, not_last))
    def _():
        wait_sent(up_out, up_in, up_sems, layer - 1)


def tile_copy(source, target, send, recv, k, tiles, layer, tile):
    return pltpu.make_async_remote_copy(
        src_ref=source, dst_ref=target.at[tile], send_sem=send.at[k], recv_sem=recv.at[k],
        device_id=(layer, lax.rem(tile + k, tiles)), device_id_type=MESH,
    )


def layer_copy(source, target, send, recv, k, layers, layer, tile):
    return pltpu.make_async_remote_copy(
        src_ref=source, dst_ref=target.at[layer], send_sem=send.at[k], recv_sem=recv.at[k],
        device_id=(lax.rem(layer + k, layers), tile), device_id_type=MESH,
    )


def basis_kernel(total_rows, snap, gram, basis, triangle, lower_inv):
    order = triangle.shape[0]

    @pl.when(jnp.logical_and(pl.program_id(0) == 0, pl.program_id(1) == 0))
    def _():
        row_no = lax.broadcasted_iota(jnp.int32, gram.shape, 0)
        col_no = lax.broadcasted_iota(jnp.int32, gram.shape, 1)
        work = jnp.where(col_no < order, gram[...] / total_rows, 0.0)
        work = jnp.where(col_no == row_no + order, 1.0, work)
        for k in range(order):
            line = work[k : k + 1, :] / work[k : k + 1, k : k + 1]
            column = work[:, k : k + 1]
            work = jnp.where(row_no > k, work - column * line, work)
        diagonal = jnp.sum(jnp.where(col_no == row_no, work, 0.0), axis=1, keepdims=True)
        work = work / jnp.sqrt(diagonal)
        triangle[...] = jnp.where(col_no >= row_no, work, 0.0)[:, :order]
        lower_inv[...] = work[:, order : 2 * order]

    factor = lower_inv[...]
    for row in range(basis.shape[3]):
        basis[0, :, 0, row, :] = jnp.dot(
            factor, snap[0, row], precision=lax.Precision.HIGHEST,
            preferred_element_type=jnp.float32,
        )


def per_device(source_modes, port_cells, frequencies, layer_inverse, coupling_self, coupling_curl):
    layers = lax.axis_size("layer")
    tiles = lax.axis_size("tile")
    ports = source_modes.shape[1]
    rows = source_modes.shape[3]
    plane_width = source_modes.shape[4]
    order = ports * frequencies.shape[0] * 2
    groups = GROUPS
    width = order // groups
    vmem = pl.BlockSpec(memory_space=pltpu.VMEM)
    smem = pl.BlockSpec(memory_space=pltpu.SMEM)
    dma = pltpu.SemaphoreType.DMA
    bf16, f32 = jnp.bfloat16, jnp.float32
    halo_shape = (groups, rows + 2, 2, width, plane_width)
    field_shape = (groups, rows, 2, width, plane_width)
    snap, gram = pl.pallas_call(
        functools.partial(sweep_kernel, layers, tiles),
        out_shape=(
            jax.ShapeDtypeStruct((2, rows, order, plane_width), f32),
            jax.ShapeDtypeStruct((order, 128), f32),
        ),
        in_specs=[smem, smem, vmem, vmem, vmem, pl.BlockSpec(memory_space=pl.ANY)],
        out_specs=(vmem, vmem),
        scratch_shapes=[
            pltpu.VMEM(layer_inverse.shape[1:], bf16),
            pltpu.VMEM(layer_inverse.shape[1:], bf16),
            pltpu.VMEM((groups, 2, rows, width, plane_width), f32),
            pltpu.VMEM(halo_shape, bf16),
            pltpu.VMEM(field_shape, bf16),
            pltpu.VMEM(halo_shape, bf16),
            pltpu.VMEM(field_shape, bf16),
            pltpu.VMEM((order, 128), f32),
            pltpu.VMEM((tiles, order, 128), f32),
            pltpu.VMEM((layers, order, 128), f32),
            pltpu.VMEM((order, 128), f32),
            dma((2, rows)),
            dma((groups, rows)), dma((groups, rows)), dma((groups, 2)), dma((groups, 2)),
            dma((groups, rows)), dma((groups, rows)), dma((groups, 2)), dma((groups, 2)),
            dma((tiles,)), dma((tiles,)), dma((layers,)), dma((layers,)),
        ],
        compiler_params=pltpu.CompilerParams(collective_id=0, has_side_effects=True),
        name="sweep",
    )(port_cells, frequencies, source_modes, coupling_self, coupling_curl, layer_inverse)
    total_rows = layers * tiles * 2 * rows * plane_width
    return pl.pallas_call(
        functools.partial(basis_kernel, total_rows),
        out_shape=(
            jax.ShapeDtypeStruct((1, order, 2, rows, plane_width), f32),
            jax.ShapeDtypeStruct((order, order), f32),
        ),
        grid=(2, SPLIT),
        in_specs=[
            pl.BlockSpec((1, rows, order, plane_width // SPLIT), lambda i, k: (i, 0, 0, k)),
            pl.BlockSpec((order, 128), lambda i, k: (0, 0)),
        ],
        out_specs=(
            pl.BlockSpec((1, order, 1, rows, plane_width // SPLIT), lambda i, k: (0, 0, i, 0, k)),
            pl.BlockSpec((order, order), lambda i, k: (0, 0)),
        ),
        scratch_shapes=[pltpu.VMEM((order, order), f32)],
        name="basis",
    )(snap, gram)


def solution(mesh):
    in_specs = (
        P("layer", None, None, "tile", None),
        P(),
        P(),
        P("layer", None, "tile", None, None),
        P("layer", None, "tile", None),
        P("layer", None, "tile", None),
    )
    out_specs = (P("layer", None, None, "tile", None), P())
    return jax.shard_map(
        per_device, mesh=mesh, in_specs=in_specs, out_specs=out_specs, check_vma=False
    )
```

```python
import functools

import jax
import jax.numpy as jnp
from jax import lax
from jax.experimental import pallas as pl
from jax.experimental.pallas import tpu as pltpu
from jax.sharding import PartitionSpec as P

MESH = pl.DeviceIdType.MESH
GROUPS = 4
TURN = 128
SPLIT = 1


def dot_last(a, b, precision=None):
    return lax.dot_general(
        a, b, (((1,), (1,)), ((), ())), precision=precision, preferred_element_type=jnp.float32
    )


def sweep_kernel(
    layers, tiles,
    port_cells, frequencies, src, self_w, curl_w, inv_hbm,
    snap, gram,
    inv, inv_t, forcing, down_in, down, up_in, up_out, gram_acc, gram_tile, gram_layer, gram_part,
    inv_sem, down_send, down_recv, down_edge_send, down_edge_recv,
    up_send, up_recv, up_edge_send, up_edge_recv,
    tile_send, tile_recv, layer_send, layer_recv,
):
    layer = lax.axis_index("layer")
    tile = lax.axis_index("tile")
    groups, rows = down.shape[0], down.shape[1]
    width = down.shape[3]
    last = rows - 1
    odd = lax.rem(tile, 2)
    sign = 1 - 2 * odd
    front = tile - sign
    back = tile + sign
    has_front = jnp.logical_and(front >= 0, front < tiles)
    has_back = jnp.logical_and(back >= 0, back < tiles)
    partners = ((has_front, front), (has_back, back))
    top = layers - 1
    not_first = layer > 0
    not_last = layer < top

    def row_of(step):
        return step + odd * (last - 2 * step)

    def inv_copy(comp, step):
        row = row_of(step)
        return pltpu.make_async_copy(
            inv_hbm.at[0, comp, row], inv.at[comp, row], inv_sem.at[comp, step]
        )

    def start_weights(step, carry):
        inv_copy(0, step).start()
        inv_copy(1, step).start()
        return carry

    lax.fori_loop(0, rows, start_weights, 0)

    barrier = pltpu.get_barrier_semaphore()

    def greet(dev_layer, dev_tile):
        pl.semaphore_signal(barrier, inc=1, device_id=(dev_layer, dev_tile), device_id_type=MESH)

    for shift in (-1, 1):
        near = layer + shift
        ok = jnp.logical_and(near >= 0, near < layers)
        for has, partner in partners:
            @pl.when(jnp.logical_and(ok, has))
            def _(near=near, partner=partner):
                greet(near, partner)

    for k in range(1, layers):
        greet(lax.rem(layer + k, layers), tile)
    for k in range(1, tiles):
        greet(layer, lax.rem(tile + k, tiles))

    plane_width = src.shape[4]
    row_no = lax.broadcasted_iota(jnp.int32, (width, plane_width), 0)
    lane = lax.broadcasted_iota(jnp.int32, (width, plane_width), 1)
    port_count = src.shape[1] // groups
    port_cols = width // port_count
    column = lane.astype(jnp.float32)
    in_port = lax.rem(row_no, port_cols)
    pitch = (layer + 1).astype(jnp.float32)
    angle = jnp.full((width, plane_width), frequencies[0] * pitch)
    for k in range(1, port_cols // 2):
        angle = jnp.where(in_port >= 2 * k, frequencies[k] * pitch, angle)
    phase = jnp.where(lax.rem(in_port, 2) == 0, jnp.cos(angle), jnp.sin(angle))

    def make_forcing(group, carry):
        centre = jnp.full((width, plane_width), port_cells[port_count * group].astype(jnp.float32))
        for k in range(1, port_count):
            cell = port_cells[port_count * group + k].astype(jnp.float32)
            centre = jnp.where(row_no >= k * port_cols, cell, centre)
        offset = (column - centre) / (plane_width // 8)
        scale = phase * (1.0 / (1.0 + offset * offset))
        for comp in range(2):
            modes = [src[0, port_count * group + k, comp].astype(jnp.float32) for k in range(port_count)]
            for row in range(rows):
                mixed = jnp.broadcast_to(modes[0][row : row + 1], scale.shape)
                for k in range(1, port_count):
                    mixed = jnp.where(row_no >= k * port_cols, modes[k][row : row + 1], mixed)
                forcing[group, comp, row] = mixed * scale
        return carry

    lax.fori_loop(0, groups, make_forcing, 0)

    @pl.when(layer == 0)
    def _():
        def clear(group, carry):
            down_in[group] = jnp.zeros(down_in.shape[1:], down_in.dtype)
            return carry

        lax.fori_loop(0, groups, clear, 0)

    for edge, (has, _) in enumerate(partners):
        slot = 0 if edge == 0 else rows + 1

        @pl.when(jnp.logical_not(has))
        def _(slot=slot):
            def clear(group, carry):
                down_in[group, slot, 1] = jnp.zeros(down_in.shape[3:], down_in.dtype)
                up_in[group, slot, 1] = jnp.zeros(up_in.shape[3:], up_in.dtype)
                return carry

            lax.fori_loop(0, groups, clear, 0)

    gram_acc[...] = jnp.zeros_like(gram_acc)

    sides = (layer > 0).astype(jnp.int32) + (layer < top).astype(jnp.int32)
    fronts = has_front.astype(jnp.int32) + has_back.astype(jnp.int32)
    pl.semaphore_wait(barrier, layers - 1 + tiles - 1 + sides * fronts)

    def main_copy(source, target, sems, group, step, near):
        return pltpu.make_async_remote_copy(
            src_ref=source.at[group, step], dst_ref=target.at[group, step + 1],
            send_sem=sems[0].at[group, step], recv_sem=sems[1].at[group, step],
            device_id=(near, tile), device_id_type=MESH,
        )

    def edge_copy(source, target, sems, group, edge, near):
        step, slot = (0, 0) if edge == 0 else (last, rows + 1)
        return pltpu.make_async_remote_copy(
            src_ref=source.at[group, step, 1], dst_ref=target.at[group, slot, 1],
            send_sem=sems[2].at[group, edge], recv_sem=sems[3].at[group, edge],
            device_id=(near, partners[edge][1]), device_id_type=MESH,
        )

    def send_unit(source, target, sems, group, step, near):
        main_copy(source, target, sems, group, step, near).start()
        for edge, at in ((0, 0), (1, last)):
            @pl.when(jnp.logical_and(step == at, partners[edge][0]))
            def _(edge=edge):
                edge_copy(source, target, sems, group, edge, near).start()

    def wait_unit(source, target, sems, group, step, near):
        @pl.when(step == 0)
        def _():
            main_copy(source, target, sems, group, 0, near).wait_recv()

            @pl.when(has_front)
            def _():
                edge_copy(source, target, sems, group, 0, near).wait_recv()

        @pl.when(step < last)
        def _():
            main_copy(source, target, sems, group, step + 1, near).wait_recv()

        @pl.when(jnp.logical_and(step == last, has_back))
        def _():
            edge_copy(source, target, sems, group, 1, near).wait_recv()

    def wait_sent(source, target, sems, near):
        def group_body(group, carry):
            def step_body(step, inner):
                main_copy(source, target, sems, group, step, near).wait_send()
                return inner

            lax.fori_loop(0, rows, step_body, 0)
            for edge in range(2):
                @pl.when(partners[edge][0])
                def _(edge=edge):
                    edge_copy(source, target, sems, group, edge, near).wait_send()

            return carry

        lax.fori_loop(0, groups, group_body, 0)

    down_sems = (down_send, down_recv, down_edge_send, down_edge_recv)
    up_sems = (up_send, up_recv, up_edge_send, up_edge_recv)
    sign_f = sign.astype(jnp.float32)

    def couple(field, group, step, row):
        x_part = field[group, step + 1, 0].astype(jnp.float32)
        y_part = field[group, step + 1, 1].astype(jnp.float32)
        before = field[group, step, 1].astype(jnp.float32)
        after = field[group, step + 2, 1].astype(jnp.float32)
        row_diff = sign_f * (after - before)
        right = jnp.where(lane == plane_width - 1, 0.0, pltpu.roll(x_part, plane_width - 1, 1))
        left = jnp.where(lane == 0, 0.0, pltpu.roll(x_part, 1, 1))
        at = pl.ds(row, 1)
        part_one = self_w[0, 0, at, :] * x_part + curl_w[0, 0, at, :] * row_diff
        part_two = self_w[0, 1, at, :] * y_part + curl_w[0, 1, at, :] * (right - left)
        return part_one, part_two

    def columns_of(group):
        return pl.ds(pl.multiple_of(group * width, width), width)

    def add_gram(group, row):
        @pl.when(group == groups - 1)
        def _():
            for comp in range(2):
                block = snap[comp, row]
                gram_acc[:, : block.shape[0]] += dot_last(block, block, lax.Precision.HIGHEST)

    def turn_block(comp, row):
        for at in range(0, plane_width, TURN):
            for to in range(0, plane_width, TURN):
                block = inv[comp, row, at : at + TURN, to : to + TURN]
                inv_t[comp, row, to : to + TURN, at : at + TURN] = block.T

    def apply_turned(vectors, comp, row):
        return jnp.dot(vectors, inv_t[comp, row], preferred_element_type=jnp.float32)

    def down_unit(opening, group, step):
        row = row_of(step)

        @pl.when(not_first)
        def _():
            wait_unit(down, down_in, down_sems, group, step, layer - 1)

        if opening:
            inv_copy(0, step).wait()
            inv_copy(1, step).wait()

        parts = couple(down_in, group, step, row)
        fields = []
        for comp in range(2):
            residue = (forcing[group, comp, row] - parts[comp]).astype(jnp.bfloat16)
            if opening:
                field = dot_last(residue, inv[comp, row]).astype(jnp.bfloat16)
            else:
                field = apply_turned(residue, comp, row).astype(jnp.bfloat16)
            down[group, step, comp] = field
            fields.append(field)
        if opening:
            for comp in range(2):
                turn_block(comp, row)

        @pl.when(not_last)
        def _():
            send_unit(down, down_in, down_sems, group, step, layer + 1)

        @pl.when(layer == top)
        def _():
            if layers > 1:
                send_unit(down, up_in, up_sems, group, step, layer - 1)
            for comp in range(2):
                snap[comp, row, columns_of(group), :] = fields[comp].astype(jnp.float32)
            add_gram(group, row)

    def up_unit(group, step):
        row = row_of(step)
        wait_unit(up_out, up_in, up_sems, group, step, layer + 1)
        parts = couple(up_in, group, step, row)
        for comp in range(2):
            image = parts[comp].astype(jnp.bfloat16)
            update = apply_turned(image, comp, row)
            value = down[group, step, comp].astype(jnp.float32) - update
            snap[comp, row, columns_of(group), :] = value
            up_out[group, step, comp] = value.astype(jnp.bfloat16)

        @pl.when(not_first)
        def _():
            send_unit(up_out, up_in, up_sems, group, step, layer - 1)

        add_gram(group, row)

    def run(unit, first):
        def group_body(group, carry):
            def step_body(step, inner):
                unit(group, step)
                return inner

            return lax.fori_loop(0, rows, step_body, carry)

        lax.fori_loop(first, groups, group_body, 0)

    def open_body(step, carry):
        down_unit(True, 0, step)
        return carry

    lax.fori_loop(0, rows, open_body, 0)
    run(functools.partial(down_unit, False), 1)

    @pl.when(not_last)
    def _():
        run(up_unit, 0)

    gram_tile[tile] = gram_acc[...]
    for k in range(1, tiles):
        tile_copy(gram_acc, gram_tile, tile_send, tile_recv, k, tiles, layer, tile).start()
    for k in range(1, tiles):
        tile_copy(gram_acc, gram_tile, tile_send, tile_recv, k, tiles, layer, tile).wait_recv()
    gram_part[...] = functools.reduce(lambda a, b: a + b, [gram_tile[k] for k in range(tiles)])
    gram_layer[layer] = gram_part[...]
    for k in range(1, layers):
        layer_copy(gram_part, gram_layer, layer_send, layer_recv, k, layers, layer, tile).start()
    for k in range(1, layers):
        layer_copy(gram_part, gram_layer, layer_send, layer_recv, k, layers, layer, tile).wait_recv()
    gram[...] = functools.reduce(lambda a, b: a + b, [gram_layer[k] for k in range(layers)])

    for k in range(1, tiles):
        tile_copy(gram_acc, gram_tile, tile_send, tile_recv, k, tiles, layer, tile).wait_send()
    for k in range(1, layers):
        layer_copy(gram_part, gram_layer, layer_send, layer_recv, k, layers, layer, tile).wait_send()

    @pl.when(not_last)
    def _():
        wait_sent(down, down_in, down_sems, layer + 1)

    if layers > 1:
        @pl.when(layer == top)
        def _():
            wait_sent(down, up_in, up_sems, layer - 1)

    @pl.when(jnp.logical_and(not_first, not_last))
    def _():
        wait_sent(up_out, up_in, up_sems, layer - 1)


def tile_copy(source, target, send, recv, k, tiles, layer, tile):
    return pltpu.make_async_remote_copy(
        src_ref=source, dst_ref=target.at[tile], send_sem=send.at[k], recv_sem=recv.at[k],
        device_id=(layer, lax.rem(tile + k, tiles)), device_id_type=MESH,
    )


def layer_copy(source, target, send, recv, k, layers, layer, tile):
    return pltpu.make_async_remote_copy(
        src_ref=source, dst_ref=target.at[layer], send_sem=send.at[k], recv_sem=recv.at[k],
        device_id=(lax.rem(layer + k, layers), tile), device_id_type=MESH,
    )


def basis_kernel(total_rows, snap, gram, basis, triangle, lower_inv):
    order = triangle.shape[0]

    @pl.when(jnp.logical_and(pl.program_id(0) == 0, pl.program_id(1) == 0))
    def _():
        row_no = lax.broadcasted_iota(jnp.int32, gram.shape, 0)
        col_no = lax.broadcasted_iota(jnp.int32, gram.shape, 1)
        work = jnp.where(col_no < order, gram[...] / total_rows, 0.0)
        work = jnp.where(col_no == row_no + order, 1.0, work)
        for k in range(order):
            line = work[k : k + 1, :] / work[k : k + 1, k : k + 1]
            column = work[:, k : k + 1]
            work = jnp.where(row_no > k, work - column * line, work)
        diagonal = jnp.sum(jnp.where(col_no == row_no, work, 0.0), axis=1, keepdims=True)
        work = work / jnp.sqrt(diagonal)
        triangle[...] = jnp.where(col_no >= row_no, work, 0.0)[:, :order]
        lower_inv[...] = work[:, order : 2 * order]

    factor = lower_inv[...]
    for row in range(basis.shape[3]):
        basis[0, :, 0, row, :] = jnp.dot(
            factor, snap[0, row], precision=lax.Precision.HIGHEST,
            preferred_element_type=jnp.float32,
        )


def per_device(source_modes, port_cells, frequencies, layer_inverse, coupling_self, coupling_curl):
    layers = lax.axis_size("layer")
    tiles = lax.axis_size("tile")
    ports = source_modes.shape[1]
    rows = source_modes.shape[3]
    plane_width = source_modes.shape[4]
    order = ports * frequencies.shape[0] * 2
    groups = GROUPS
    width = order // groups
    vmem = pl.BlockSpec(memory_space=pltpu.VMEM)
    smem = pl.BlockSpec(memory_space=pltpu.SMEM)
    dma = pltpu.SemaphoreType.DMA
    bf16, f32 = jnp.bfloat16, jnp.float32
    halo_shape = (groups, rows + 2, 2, width, plane_width)
    field_shape = (groups, rows, 2, width, plane_width)
    snap, gram = pl.pallas_call(
        functools.partial(sweep_kernel, layers, tiles),
        out_shape=(
            jax.ShapeDtypeStruct((2, rows, order, plane_width), f32),
            jax.ShapeDtypeStruct((order, 128), f32),
        ),
        in_specs=[smem, smem, vmem, vmem, vmem, pl.BlockSpec(memory_space=pl.ANY)],
        out_specs=(vmem, vmem),
        scratch_shapes=[
            pltpu.VMEM(layer_inverse.shape[1:], bf16),
            pltpu.VMEM(layer_inverse.shape[1:], bf16),
            pltpu.VMEM((groups, 2, rows, width, plane_width), f32),
            pltpu.VMEM(halo_shape, bf16),
            pltpu.VMEM(field_shape, bf16),
            pltpu.VMEM(halo_shape, bf16),
            pltpu.VMEM(field_shape, bf16),
            pltpu.VMEM((order, 128), f32),
            pltpu.VMEM((tiles, order, 128), f32),
            pltpu.VMEM((layers, order, 128), f32),
            pltpu.VMEM((order, 128), f32),
            dma((2, rows)),
            dma((groups, rows)), dma((groups, rows)), dma((groups, 2)), dma((groups, 2)),
            dma((groups, rows)), dma((groups, rows)), dma((groups, 2)), dma((groups, 2)),
            dma((tiles,)), dma((tiles,)), dma((layers,)), dma((layers,)),
        ],
        compiler_params=pltpu.CompilerParams(collective_id=0, has_side_effects=True),
        name="sweep",
    )(port_cells, frequencies, source_modes, coupling_self, coupling_curl, layer_inverse)
    total_rows = layers * tiles * 2 * rows * plane_width
    return pl.pallas_call(
        functools.partial(basis_kernel, total_rows),
        out_shape=(
            jax.ShapeDtypeStruct((1, order, 2, rows, plane_width), f32),
            jax.ShapeDtypeStruct((order, order), f32),
        ),
        grid=(2, SPLIT),
        in_specs=[
            pl.BlockSpec((1, rows, order, plane_width // SPLIT), lambda i, k: (i, 0, 0, k)),
            pl.BlockSpec((order, 128), lambda i, k: (0, 0)),
        ],
        out_specs=(
            pl.BlockSpec((1, order, 1, rows, plane_width // SPLIT), lambda i, k: (0, 0, i, 0, k)),
            pl.BlockSpec((order, order), lambda i, k: (0, 0)),
        ),
        scratch_shapes=[pltpu.VMEM((order, order), f32)],
        name="basis",
    )(snap, gram)


def solution(mesh):
    in_specs = (
        P("layer", None, None, "tile", None),
        P(),
        P(),
        P("layer", None, "tile", None, None),
        P("layer", None, "tile", None),
        P("layer", None, "tile", None),
    )
    out_specs = (P("layer", None, None, "tile", None), P())
    return jax.shard_map(
        per_device, mesh=mesh, in_specs=in_specs, out_specs=out_specs, check_vma=False
    )
```
